256 devices in a mesh: seq: 32 (over x, z), tp: 8 (over y, core).
Axes of the slice: x: 4, y: 4, z: 8, core: 2. Of those that a mesh axis runs over, the one named last changes fastest.
Arguments:
- event_vectors: bfloat16 [16384, 6144], P('seq'), may hold values from -6 to 6
- question_projector: bfloat16 [6144, 4096], P('seq', 'tp'), may hold values from -0.078125 to 0.078125
- lookup_projector: bfloat16 [6144, 4096], P('seq', 'tp'), may hold values from -0.078125 to 0.078125
- content_projector: bfloat16 [6144, 4096], P('seq', 'tp'), may hold values from -0.078125 to 0.078125
- channel_fading_speed: float32 [32], P('tp'), may hold values from 1.2207031e-05 to 0.03334
- surge_fading: float32 [16384], P('seq'), may hold values from -0.6932 to 0, as said below
- channel_scaling_coefficient: float32 [4096], P('tp'), may hold values from 0.1 to 1.9
- final_projector: bfloat16 [4096, 6144], P('seq', 'tp'), may hold values from -0.09375 to 0.09375
Outputs:
- mixed: bfloat16 [16384, 6144], P('seq', 'tp')
The draws below stay inside these ranges and needn't reach their ends.
Inputs may be any that keep to these rules, and one draw needn't show every extreme that they name: `surge_fading`: zero at all but a few positions of the sequence.
All inputs are finite; a program needn't handle non-finite values.
Results may differ from the reference program's by a relative error of at most 0.0063.
Values may be sent and summed in bfloat16 or wider, within the bound.
A program may use at most 128 MiB of HBM per device.

```python
import jax
import jax.numpy as jnp
from jax import lax

D = 6144
SHARD_CHANNELS = 32
HD = 128
SPAN_LENGTH = 512
TOKENS = 16384
HF = 4096


def draw_channel_fading_speed(key, part):
    key_pick, key_slow, key_fast = jax.random.split(jax.random.fold_in(key, 11), 3)
    share = 0.5
    picked = jax.random.uniform(key_pick, (SHARD_CHANNELS,), jnp.float32) < share
    slow_rate = jnp.exp(jax.random.uniform(key_slow, (SHARD_CHANNELS,), jnp.float32, jnp.log(0.2), jnp.log(2.0))) / TOKENS
    fast_rate = jnp.exp(jax.random.uniform(key_fast, (SHARD_CHANNELS,), jnp.float32, jnp.log(1.0 / 50.0), jnp.log(1.0 / 30.0)))
    return jnp.where(picked, slow_rate, fast_rate).astype(jnp.float32)


def draw_surge_fading(key, part):
    key_spot, key_depth = jax.random.split(jax.random.fold_in(key, 23), 2)
    spots = jax.random.randint(key_spot, (8,), 0, TOKENS)
    depth = jnp.log(jax.random.uniform(key_depth, (8,), jnp.float32, 0.5, 0.8))
    return jnp.zeros((TOKENS,), jnp.float32).at[spots].set(depth)


def block_levels(own_key, shape, shards, least, largest):
    loudness = 1.0
    for dim, parts in shards:
        heights = jax.random.uniform(jax.random.fold_in(jax.random.fold_in(own_key, 6), dim), (parts,), jnp.float32, least / len(shards), largest / len(shards))
        loudness = loudness * jnp.repeat(jnp.exp(heights), shape[dim] // parts).reshape((-1,) + (1,) * (len(shape) - 1 - dim))
    return loudness


def noise(rng, shape, deviation, limit, cuts=(), kind=jnp.bfloat16):
    drawn = jax.random.normal(rng, shape, jnp.float32) * deviation
    if len(cuts) > 0:
        drawn = block_levels(rng, shape, cuts, -0.22, 0.18) * drawn
    return jnp.clip(drawn, min=-limit, max=limit).astype(kind)


def setup_inputs(seed: int = 0) -> dict:
    seeds = jax.random.split(jax.random.key(seed), 9)
    event_vectors = noise(seeds[0], (TOKENS, D), 1.0, 6.0, ((0, 32),))
    question_projector = noise(seeds[1], (D, HF), D ** -0.5, 0.078125, ((0, 32), (1, 8)))
    lookup_projector = noise(seeds[2], (D, HF), D ** -0.5, 0.078125, ((0, 32), (1, 8)))
    content_projector = noise(seeds[3], (D, HF), D ** -0.5, 0.078125, ((0, 32), (1, 8)))
    channel_fading_speed = draw_channel_fading_speed(jax.random.fold_in(seeds[8], 71), 0)
    surge_fading = draw_surge_fading(jax.random.fold_in(seeds[8], 71), 0)
    channel_scaling_coefficient = jnp.clip(1.0 + 0.18 * jax.random.normal(seeds[6], (HF,), jnp.float32), 0.1, 1.9)
    final_projector = noise(seeds[7], (HF, D), HF ** -0.5, 0.09375, ((0, 32), (1, 8)))
    return {"event_vectors": event_vectors, "question_projector": question_projector, "lookup_projector": lookup_projector, "content_projector": content_projector, "channel_fading_speed": channel_fading_speed, "surge_fading": surge_fading, "channel_scaling_coefficient": channel_scaling_coefficient, "final_projector": final_projector}


def block_pass(carry, inputs):
    carried = carry
    query_block, key_block, value_block, log_block = inputs
    inside = jnp.cumsum(log_block, axis=0)
    block_total = inside[-1]
    highest = lax.Precision.HIGHEST
    scores = jnp.einsum('thd,shd->hts', query_block, key_block, precision=highest)
    spread_log = inside.T[:, :, None] - inside.T[:, None, :]
    rows_index = lax.broadcasted_iota(jnp.int32, (SPAN_LENGTH, SPAN_LENGTH), 0)
    cols_index = lax.broadcasted_iota(jnp.int32, (SPAN_LENGTH, SPAN_LENGTH), 1)
    causal = (rows_index >= cols_index)[None, :, :]
    weight = jnp.where(causal, jnp.exp(jnp.where(causal, spread_log, 0.0)), 0.0)
    within = jnp.einsum('hts,shd->thd', scores * weight, value_block, precision=highest)
    across = jnp.einsum('thd,hde->the', query_block * jnp.exp(inside)[:, :, None], carried, precision=highest)
    updated = jnp.exp(block_total)[:, None, None] * carried + jnp.einsum('shd,she->hde', key_block * jnp.exp(block_total[None, :] - inside)[:, :, None], value_block, precision=highest)
    return (updated, within + across)

def reference(event_vectors, question_projector, lookup_projector, content_projector, channel_fading_speed, surge_fading, channel_scaling_coefficient, final_projector):
    queries = jax.nn.silu(jnp.dot(event_vectors, question_projector, preferred_element_type=jnp.float32)).astype(jnp.bfloat16)
    keys_act = jax.nn.silu(jnp.dot(event_vectors, lookup_projector, preferred_element_type=jnp.float32)).astype(jnp.bfloat16)
    values_act = jnp.dot(event_vectors, content_projector, preferred_element_type=jnp.float32).astype(jnp.bfloat16)
    span_count = TOKENS // SPAN_LENGTH
    shaped = (span_count, SPAN_LENGTH, SHARD_CHANNELS, HD)
    query_blocks = queries.astype(jnp.float32).reshape(shaped)
    key_blocks = keys_act.astype(jnp.float32).reshape(shaped)
    value_blocks = values_act.astype(jnp.float32).reshape(shaped)
    stepwise_fading_exponent = (surge_fading[:, None] - channel_fading_speed[None, :]).reshape((span_count, SPAN_LENGTH, SHARD_CHANNELS))
    start_state = jnp.zeros((SHARD_CHANNELS, HD, HD), jnp.float32)
    final_state, outputs = lax.scan(block_pass, start_state, (query_blocks, key_blocks, value_blocks, stepwise_fading_exponent))
    attention = outputs.reshape((TOKENS, SHARD_CHANNELS, HD))
    meansq = lax.optimization_barrier(jnp.mean(attention * attention, axis=-1, keepdims=True))
    normed = attention / jnp.sqrt(meansq + 1e-05) * channel_scaling_coefficient.reshape((SHARD_CHANNELS, HD))[None, :, :]
    normed = normed.reshape((TOKENS, SHARD_CHANNELS * HD)).astype(jnp.bfloat16)
    return jnp.dot(normed, final_projector, preferred_element_type=jnp.float32).astype(jnp.bfloat16)
```

```python
import jax
import jax.numpy as jnp
from jax import lax
from jax.experimental import pallas as pl
from jax.experimental.pallas import tpu as pltpu
from jax.sharding import PartitionSpec as P

MESH = pl.DeviceIdType.MESH
F32 = jnp.float32
BF16 = jnp.bfloat16
NZ = 8
NY = 4
PIECES = 2
COPIES = 220


def aligned(value, by):
    return pl.multiple_of(value, by)


def kernel(
    x_hbm, wq_hbm, wk_hbm, wv_hbm, wo_hbm, aux_hbm, out_ref,
    xs, wk, wv, wq, wo, acc, part, kb, vb, qb, decay, aux,
    states, arrived, totals, tot_out, group_out, groups, prefix_out, prefix,
    normed, staged, oacc, ssem, rsem, lsem,
):
    s = lax.axis_index("seq")
    t = lax.axis_index("tp")
    x, z = s // NZ, s % NZ
    y, c = t // 2, t % 2
    region = x // 2
    is_home = 1 - (region + c) % 2
    xe = 3 - x
    xi = x + 1 - 2 * (x % 2)
    xt = is_home * x + (1 - is_home) * xe
    p = xt % 2
    home = is_home == 1
    away = is_home == 0

    def dev(cx, cy, cz, cc):
        return (cx * NZ + cz, cy * 2 + cc)

    z_dev = [dev(x, y, (z + d) % NZ, c) for d in range(NZ)]
    up, down = z_dev[1], z_dev[NZ - 1]
    inner = dev(xi, y, z, c)
    inner_other = dev(xi, y, z, 1 - c)
    across_chip = dev(xe, y, z, c)
    swap = dev(xe, y, z, 1 - c)
    other = dev(x, y, z, 1 - c)
    y_up = dev(x, (y + 1) % NY, z, c)
    y_down = dev(x, (y + 3) % NY, z, c)
    peers = z_dev[1:] + [inner, inner_other, across_chip, swap, other, y_up, y_down]

    used = [0]
    sent = []
    sent_away = []

    def remote(src, dst, device):
        i = used[0]
        used[0] += 1
        return pltpu.make_async_remote_copy(
            src_ref=src, dst_ref=dst, send_sem=ssem.at[i], recv_sem=rsem.at[i],
            device_id=device, device_id_type=MESH,
        )

    def send(src, dst, device):
        copy = remote(src, dst, device)
        copy.start()
        sent.append(copy)
        return copy

    barrier = pltpu.get_barrier_semaphore()
    for device in peers:
        pl.semaphore_signal(barrier, inc=1, device_id=device, device_id_type=MESH)
    pl.semaphore_wait(barrier, len(peers))

    own_row = aligned(192 * (p * NZ + z), 64)
    source_row = aligned(192 * ((x % 2) * NZ + z), 64)
    swaps = {}

    def own_piece(name, src, dst, index):
        local = pltpu.make_async_copy(src, dst, lsem.at[index])
        copy = remote(src, dst, swap)
        swaps[name] = (local, copy)

        @pl.when(home)
        def _():
            local.start()

        @pl.when(away)
        def _():
            copy.start()

        sent_away.append(copy)

    def wait_own(name):
        local, copy = swaps[name]

        @pl.when(home)
        def _():
            local.wait()

        @pl.when(away)
        def _():
            copy.wait_recv()

    own_piece("k", wk_hbm, wk.at[pl.ds(source_row, 192)], 0)
    own_piece("v", wv_hbm, wv.at[pl.ds(source_row, 192)], 1)
    own_piece("aux", aux_hbm, aux, 2)
    half_lane = aligned(3072 * c, 128)
    quarter = aligned(128 * y, 128)
    x_cross = send(
        x_hbm.at[pl.ds(quarter, 128), pl.ds(half_lane, 3072)],
        xs.at[region, pl.ds(quarter, 128)], across_chip,
    )
    own_piece("q", wq_hbm, wq.at[pl.ds(source_row, 192)], 3)
    x_local = pltpu.make_async_copy(x_hbm.at[:, pl.ds(half_lane, 3072)], xs.at[region], lsem.at[4])
    x_local.start()
    o_own_row = aligned(128 * s, 128)
    o_local = pltpu.make_async_copy(wo_hbm, wo.at[pl.ds(o_own_row, 128)], lsem.at[5])
    o_local.start()

    class Round:
        def __init__(self, own_x, nbr_x, own_z, hops):
            self.own_x, self.nbr_x, self.own_z = own_x, nbr_x, own_z
            self.parts = {"a": own_x, "b": nbr_x, "z": own_z}
            self.hops = hops
            self.ring = {}
            self.side = []

        def begin_flow(self, f):
            part = self.parts[f](z)
            self.ring[f, 0, 1] = send(part, part, up)
            self.ring[f, 1, 1] = send(part, part, down)

        def start(self):
            own = self.own_x(z)
            self.first = send(own, own, inner)
            self.begin_flow("a")
            self.begin_flow("z")
            own = self.own_z(z)
            self.side.append((0, send(own, own, inner)))

        def start_nbr(self):
            self.first.wait_recv()
            self.begin_flow("b")

        def step(self, d):
            for f in ("a", "z", "b"):
                for way in (0, 1):
                    limit = self.hops[f][way]
                    if d > limit:
                        continue
                    self.ring[f, way, d].wait_recv()
                    where = (z + NZ - d) % NZ if way == 0 else (z + d) % NZ
                    part = self.parts[f](where)
                    if d < limit:
                        self.ring[f, way, d + 1] = send(part, part, up if way == 0 else down)
                    if f == "z":
                        self.side.append((d, send(part, part, inner)))

        def wait_side(self, low, high):
            for d, copy in self.side:
                if low <= d <= high:
                    copy.wait_recv()

    def rows(ref, start, count, by):
        return ref.at[pl.ds(aligned(start, by), count)]

    kv = Round(
        lambda w: rows(wk, 192 * (p * NZ + w), 192, 64),
        lambda w: rows(wk, 192 * ((1 - p) * NZ + w), 192, 64),
        lambda w: rows(wv, 192 * (p * NZ + w), 192, 64),
        {"a": (4, 3), "b": (3, 4), "z": (4, 3)},
    )
    qr = Round(
        lambda w: rows(wq, 192 * (p * NZ + w), 96, 32),
        lambda w: rows(wq, 192 * ((1 - p) * NZ + w), 96, 32),
        lambda w: rows(wq, 192 * (p * NZ + w) + 96, 96, 32),
        {"a": (4, 3), "b": (3, 4), "z": (3, 4)},
    )
    orr = Round(
        lambda w: rows(wo, 128 * (x * NZ + w), 128, 128),
        lambda w: rows(wo, 128 * (xi * NZ + w), 128, 128),
        lambda w: rows(wo, 128 * (xe * NZ + w), 128, 128),
        {"a": (4, 3), "b": (3, 4), "z": (3, 4)},
    )

    weights = {0: wk, 1: wv, 2: wq}
    last_pair = ((z + 4) % NZ) // 2

    def mm_chunk(which, pair):
        low = aligned(384 * pair, 128)
        high = aligned(1536 + 384 * pair, 128)
        for i in which:
            w = weights[i]
            wcat = jnp.concatenate([w[pl.ds(low, 384)], w[pl.ds(high, 384)]], axis=0)
            for j in (0, 1):
                xcat = jnp.concatenate([xs[j, :, pl.ds(low, 384)], xs[j, :, pl.ds(high, 384)]], axis=1)
                acc[i, j] += jnp.dot(xcat, wcat, preferred_element_type=F32)

    def mm_three(which):
        @pl.loop(0, 3)
        def _(m):
            mm_chunk(which, (last_pair + 1 + m) % 4)

    wait_own("k")
    wait_own("v")
    kv.start()
    acc[...] = jnp.zeros_like(acc)
    kv.start_nbr()
    x_local.wait()

    wait_own("aux")
    t_col = lax.broadcasted_iota(jnp.int32, (512, 128), 0)
    lane = lax.broadcasted_iota(jnp.int32, (512, 128), 1)
    cs = jnp.zeros((512, 1), F32)
    for b in range(4):
        surge = jnp.broadcast_to(aux[b : b + 1, :], (512, 128))
        cs += jnp.sum(jnp.where(lane + 128 * b <= t_col, surge, 0.0), axis=1, keepdims=True)
    cs_row = jnp.broadcast_to(cs, (512, 128)).T[0:1, :]
    total = cs[511:512, :]
    steps = lax.broadcasted_iota(jnp.int32, (512, 1), 0).astype(F32)
    t_idx = lax.broadcasted_iota(jnp.int32, (512, 512), 0)
    s_idx = lax.broadcasted_iota(jnp.int32, (512, 512), 1)
    causal = t_idx >= s_idx
    apart = (t_idx - s_idx).astype(F32)
    spread = jnp.broadcast_to(cs, (512, 512)) - jnp.broadcast_to(cs_row, (512, 512))
    for h in range(4):
        speed = aux[8 + h : 9 + h, 0:1]
        exponent = jnp.where(causal, spread - apart * speed, 0.0)
        decay[h] = jnp.where(causal, jnp.exp(exponent), 0.0)
    tot_out[...] = jnp.broadcast_to(total, (8, 128))
    totals[z] = jnp.broadcast_to(total, (8, 128))
    tot_copies = [send(tot_out, totals.at[z], z_dev[d]) for d in range(1, NZ)]

    kv.step(1)
    wait_own("q")

    x_cross.wait_recv()
    theirs = 1 - region

    def x_rows(cy, start, count):
        return xs.at[theirs, pl.ds(aligned(128 * cy + start, 64), count)]

    own_q = x_rows(y, 0, 128)
    x_up = send(own_q, own_q, y_up)
    x_down = send(own_q, own_q, y_down)
    kv.step(2)
    x_up.wait_recv()
    far = x_rows((y + 3) % NY, 0, 64)
    x_up2 = send(far, far, y_up)
    x_down.wait_recv()
    far = x_rows((y + 1) % NY, 64, 64)
    x_down2 = send(far, far, y_down)
    o_swap_dst = wo.at[pl.ds(o_own_row, 128)]
    o_swap = send(wo_hbm, o_swap_dst, across_chip)
    kv.step(3)
    qr.start()
    x_up2.wait_recv()
    x_down2.wait_recv()
    kv.wait_side(0, 3)
    qr.start_nbr()
    mm_three((0, 1))
    kv.step(4)
    qr.step(1)
    kv.wait_side(4, 4)
    mm_chunk((0, 1), last_pair)
    k_part = send(acc.at[0, 1 - c], part.at[0], other)
    v_part = send(acc.at[1, 1 - c], part.at[1], other)
    qr.step(2)

    k_part.wait_recv()
    v_part.wait_recv()
    ksum = acc[0, c] + part[0]
    kb[...] = (ksum * (1.0 / (1.0 + jnp.exp(-ksum)))).astype(BF16)
    vb[...] = (acc[1, c] + part[1]).astype(BF16)
    for h in range(4):
        speed = aux[8 + h : 9 + h, 0:1]
        remain = jnp.exp((total - cs) - (511.0 - steps) * speed)
        kd = (kb[:, 128 * h : 128 * h + 128].astype(F32) * remain).astype(BF16)
        state = lax.dot_general(
            kd, vb[:, 128 * h : 128 * h + 128], (((0,), (0,)), ((), ())),
            preferred_element_type=F32,
        ).astype(BF16)
        states[2 * h] = state[0:64]
        states[2 * h + 1] = state[64:128]
    arrived[z] = states[z]
    state_copies = [
        send(states.at[(z + d) % NZ], arrived.at[z], z_dev[d]) for d in range(1, NZ)
    ]
    qr.step(3)
    orr_ready = [False]
    o_local.wait()
    o_swap.wait_recv()
    orr.start()
    qr.wait_side(0, 3)
    for copy in state_copies + tot_copies:
        copy.wait_recv()
    slice_speed = aux[pl.ds(8 + z // 2, 1), 0:1]
    run = jnp.zeros((64, 128), F32)
    run_tot = jnp.zeros((1, 1), F32)
    before = []
    for w in range(NZ):
        before.append((run, run_tot))
        tot = totals[w, 0:1, 0:1]
        run = jnp.exp(tot - 512.0 * slice_speed) * run + arrived[w].astype(F32)
        run_tot = run_tot + tot
    group_out[0:64, :] = run
    group_out[64:72, :] = jnp.broadcast_to(run_tot, (8, 128))
    groups[xt] = group_out[...]
    group_copies = [send(group_out, groups.at[xt], d) for d in (other, inner, inner_other)]
    mm_three((2,))
    orr.start_nbr()
    for copy in group_copies:
        copy.wait_recv()
    carry = jnp.zeros((64, 128), F32)
    for g in range(4):
        tot = groups[g, 64:65, 0:1]
        later = jnp.exp(tot - 4096.0 * slice_speed) * carry + groups[g, 0:64, :]
        carry = jnp.where(jnp.full((64, 128), g, jnp.int32) < xt, later, carry)
    for w in range(NZ):
        run, run_tot = before[w]
        prefix_out[w] = (run + jnp.exp(run_tot - (512.0 * w) * slice_speed) * carry).astype(BF16)
    prefix[z] = prefix_out[z]
    prefix_copies = [
        send(prefix_out.at[(z + d) % NZ], prefix.at[z], z_dev[d]) for d in range(1, NZ)
    ]
    qr.step(4)
    qr.wait_side(4, 4)
    mm_chunk((2,), last_pair)
    q_part = send(acc.at[2, 1 - c], part.at[2], other)
    for copy in prefix_copies:
        copy.wait_recv()
    q_part.wait_recv()
    qsum = acc[2, c] + part[2]
    qb[...] = (qsum * (1.0 / (1.0 + jnp.exp(-qsum)))).astype(BF16)

    width = 512 // PIECES
    swap_t = y * 2 + 1 - c
    swap_copies = []
    for piece in range(PIECES):
        for h in range(piece * 4 // PIECES, (piece + 1) * 4 // PIECES):
            cut = slice(128 * h, 128 * h + 128)
            speed = aux[8 + h : 9 + h, 0:1]
            q_h, k_h, v_h = qb[:, cut], kb[:, cut], vb[:, cut]
            scores = lax.dot_general(q_h, k_h, (((1,), (1,)), ((), ())), preferred_element_type=F32)
            inside = jnp.dot((scores * decay[h]).astype(BF16), v_h, preferred_element_type=F32)
            carried = prefix[2 * h : 2 * h + 2].reshape(128, 128)
            reach = jnp.exp(cs - (steps + 1.0) * speed)
            att = inside + reach * jnp.dot(q_h, carried, preferred_element_type=F32)
            square = jnp.mean(att * att, axis=1, keepdims=True)
            value = (att * lax.rsqrt(square + 1e-05) * aux[4 + h : 5 + h, :]).astype(BF16)

            @pl.when(home)
            def _():
                normed[t, :, cut] = value

            @pl.when(away)
            def _():
                staged[:, cut] = value

        lanes = pl.ds(piece * width, width)
        copy = remote(staged.at[:, lanes], normed.at[swap_t, :, lanes], swap)

        @pl.when(away)
        def _():
            copy.start()

        sent_away.append(copy)
        swap_copies.append(copy)

    orr.step(1)

    def block(cy, start, count, piece):
        return normed.at[cy * 2 + c, pl.ds(start, count), pl.ds(piece * width, width)]

    ring_up, ring_down, relays = [], [], []
    for piece in range(PIECES):
        copy = swap_copies[piece]

        @pl.when(away)
        def _():
            copy.wait_recv()

        mine = block(y, 0, 512, piece)
        ring_up.append(send(mine, mine, y_up))
        ring_down.append(send(mine, mine, y_down))
        relays.append(send(mine, mine, other))
    orr.step(2)
    ring_up2, ring_down2 = [], []
    for piece in range(PIECES):
        ring_up[piece].wait_recv()
        far = block((y + 3) % NY, 0, 256, piece)
        ring_up2.append(send(far, far, y_up))
        whole = block((y + 3) % NY, 0, 512, piece)
        relays.append(send(whole, whole, other))
        ring_down[piece].wait_recv()
        far = block((y + 1) % NY, 256, 256, piece)
        ring_down2.append(send(far, far, y_down))
        whole = block((y + 1) % NY, 0, 512, piece)
        relays.append(send(whole, whole, other))
    oacc[...] = jnp.zeros_like(oacc)
    orr.step(3)
    for piece in range(PIECES):
        ring_up2[piece].wait_recv()
        far = block((y + 2) % NY, 0, 256, piece)
        relays.append(send(far, far, other))
        ring_down2[piece].wait_recv()
        far = block((y + 2) % NY, 256, 256, piece)
        relays.append(send(far, far, other))
    orr.wait_side(0, 3)
    for copy in relays:
        copy.wait_recv()

    def out_chunk(pair):
        lanes = pl.ds(aligned(256 * (pair % 2), 128), 256)
        left = jnp.concatenate([normed[2 * g + pair // 2, :, lanes] for g in range(4)], axis=1)
        right = jnp.concatenate(
            [wo[pl.ds(aligned(1024 * g + 256 * pair, 256), 256)] for g in range(4)], axis=0
        )
        return jnp.dot(left, right, preferred_element_type=F32)

    @pl.loop(0, 3)
    def _(m):
        oacc[...] += out_chunk((last_pair + 1 + m) % 4)

    orr.step(4)
    orr.wait_side(4, 4)
    out_ref[...] = (oacc[...] + out_chunk(last_pair)).astype(BF16)

    for copy in sent:
        copy.wait_send()

    @pl.when(away)
    def _():
        for copy in sent_away:
            copy.wait_send()


def local(
    event_vectors,
    question_projector,
    lookup_projector,
    content_projector,
    channel_fading_speed,
    surge_fading,
    channel_scaling_coefficient,
    final_projector,
):
    aux = jnp.concatenate(
        [
            surge_fading.reshape(4, 128),
            channel_scaling_coefficient.reshape(4, 128),
            jnp.broadcast_to(channel_fading_speed[:, None], (4, 128)),
            jnp.zeros((4, 128), F32),
        ],
        axis=0,
    )
    return pl.pallas_call(
        kernel,
        out_shape=jax.ShapeDtypeStruct((512, 768), BF16),
        in_specs=[pl.BlockSpec(memory_space=pl.ANY)] * 6,
        out_specs=pl.BlockSpec(memory_space=pltpu.VMEM),
        scratch_shapes=[
            pltpu.VMEM((2, 512, 3072), BF16),
            pltpu.VMEM((3072, 512), BF16),
            pltpu.VMEM((3072, 512), BF16),
            pltpu.VMEM((3072, 512), BF16),
            pltpu.VMEM((4096, 768), BF16),
            pltpu.VMEM((3, 2, 512, 512), F32),
            pltpu.VMEM((3, 512, 512), F32),
            pltpu.VMEM((512, 512), BF16),
            pltpu.VMEM((512, 512), BF16),
            pltpu.VMEM((512, 512), BF16),
            pltpu.VMEM((4, 512, 512), F32),
            pltpu.VMEM((16, 128), F32),
            pltpu.VMEM((8, 64, 128), BF16),
            pltpu.VMEM((8, 64, 128), BF16),
            pltpu.VMEM((8, 8, 128), F32),
            pltpu.VMEM((8, 128), F32),
            pltpu.VMEM((72, 128), F32),
            pltpu.VMEM((4, 72, 128), F32),
            pltpu.VMEM((8, 64, 128), BF16),
            pltpu.VMEM((8, 64, 128), BF16),
            pltpu.VMEM((8, 512, 512), BF16),
            pltpu.VMEM((512, 512), BF16),
            pltpu.VMEM((512, 768), F32),
            pltpu.SemaphoreType.DMA((COPIES,)),
            pltpu.SemaphoreType.DMA((COPIES,)),
            pltpu.SemaphoreType.DMA((8,)),
        ],
        compiler_params=pltpu.CompilerParams(
            collective_id=0, has_side_effects=True, vmem_limit_bytes=67043328
        ),
    )(
        event_vectors,
        question_projector,
        lookup_projector,
        content_projector,
        final_projector,
        aux,
    )


def solution(mesh):
    in_specs = (
        P("seq", None),
        P("seq", "tp"),
        P("seq", "tp"),
        P("seq", "tp"),
        P("tp"),
        P("seq"),
        P("tp"),
        P("seq", "tp"),
    )
    out_specs = P("seq", "tp")
    return jax.shard_map(local, mesh=mesh, in_specs=in_specs, out_specs=out_specs, check_vma=False)
```

```python
import jax
import jax.numpy as jnp
from jax import lax
from jax.experimental import pallas as pl
from jax.experimental.pallas import tpu as pltpu
from jax.sharding import PartitionSpec as P

MESH = pl.DeviceIdType.MESH
F32 = jnp.float32
BF16 = jnp.bfloat16
NZ = 8
NY = 4
COPIES = 300
O_X = 48


def aligned(value, by):
    return pl.multiple_of(value, by)


def kernel(
    x_hbm, wq_hbm, wk_hbm, wv_hbm, wo_hbm, surge_ref, scale_ref, speed_ref, out_ref,
    xs, wk, wv, wq, wo, acc, part, kb, vb, qb, decay, aux, aux_own,
    states, arrived, totals, tot_out, group_out, groups, prefix_out, prefix,
    normed, staged, oacc, ssem, rsem, lsem,
):
    s = lax.axis_index("seq")
    t = lax.axis_index("tp")
    x, z = s // NZ, s % NZ
    y, c = t // 2, t % 2
    region = x // 2
    is_home = 1 - (region + c) % 2
    xe = 3 - x
    xi = x + 1 - 2 * (x % 2)
    xt = is_home * x + (1 - is_home) * xe
    p = xt % 2
    home = is_home == 1
    away = is_home == 0

    def dev(cx, cy, cz, cc):
        return (cx * NZ + cz, cy * 2 + cc)

    z_dev = [dev(x, y, (z + d) % NZ, c) for d in range(NZ)]
    up, down = z_dev[1], z_dev[NZ - 1]
    inner = dev(xi, y, z, c)
    inner_other = dev(xi, y, z, 1 - c)
    across_chip = dev(xe, y, z, c)
    swap = dev(xe, y, z, 1 - c)
    other = dev(x, y, z, 1 - c)
    y_up = dev(x, (y + 1) % NY, z, c)
    y_down = dev(x, (y + 3) % NY, z, c)
    peers = z_dev[1:] + [inner, inner_other, across_chip, swap, other, y_up, y_down]

    used = [0]
    sent = []
    sent_away = []

    def remote(src, dst, device):
        i = used[0]
        used[0] += 1
        return pltpu.make_async_remote_copy(
            src_ref=src, dst_ref=dst, send_sem=ssem.at[i], recv_sem=rsem.at[i],
            device_id=device, device_id_type=MESH,
        )

    def send(src, dst, device):
        copy = remote(src, dst, device)
        copy.start()
        sent.append(copy)
        return copy

    aux_own[0:4, :] = surge_ref[...]
    aux_own[4:8, :] = scale_ref[...]
    for h in range(4):
        aux_own[8 + h : 9 + h, :] = jnp.full((1, 128), speed_ref[h], F32)
    aux_own[12:16, :] = jnp.zeros((4, 128), F32)

    barrier = pltpu.get_barrier_semaphore()
    for device in peers:
        pl.semaphore_signal(barrier, inc=1, device_id=device, device_id_type=MESH)
    pl.semaphore_wait(barrier, len(peers))

    own_row = aligned(192 * (p * NZ + z), 64)
    source_row = aligned(192 * ((x % 2) * NZ + z), 64)
    swaps = {}

    def own_piece(name, src, dst, index):
        local = pltpu.make_async_copy(src, dst, lsem.at[index])
        copy = remote(src, dst, swap)
        swaps[name] = (local, copy)

        @pl.when(home)
        def _():
            local.start()

        @pl.when(away)
        def _():
            copy.start()

        sent_away.append(copy)

    def wait_own(name):
        local, copy = swaps[name]

        @pl.when(home)
        def _():
            local.wait()

        @pl.when(away)
        def _():
            copy.wait_recv()

    own_piece("k", wk_hbm, wk.at[pl.ds(source_row, 192)], 0)
    own_piece("v", wv_hbm, wv.at[pl.ds(source_row, 192)], 1)
    own_piece("aux", aux_own, aux, 2)
    half_lane = aligned(3072 * c, 128)
    x_cross = []
    for i in (0, 1):
        some = pl.ds(aligned(128 * y + 64 * i, 64), 64)
        x_cross.append(
            send(x_hbm.at[some, pl.ds(half_lane, 3072)], xs.at[region, some], across_chip)
        )
    own_piece("q", wq_hbm, wq.at[pl.ds(source_row, 192)], 3)
    x_local = pltpu.make_async_copy(x_hbm.at[:, pl.ds(half_lane, 3072)], xs.at[region], lsem.at[4])
    x_local.start()
    o_own_row = aligned(128 * s, 128)
    o_local = pltpu.make_async_copy(wo_hbm, wo.at[pl.ds(o_own_row, 128)], lsem.at[5])
    o_local.start()

    class Round:
        def __init__(self, own_x, nbr_x, own_z, hops):
            self.own_x, self.nbr_x, self.own_z = own_x, nbr_x, own_z
            self.parts = {"a": own_x, "b": nbr_x, "z": own_z}
            self.hops = hops
            self.ring = {}
            self.side = []

        def begin_flow(self, f):
            part = self.parts[f](z)
            self.ring[f, 0, 1] = send(part, part, up)
            self.ring[f, 1, 1] = send(part, part, down)

        def start_x(self):
            own = self.own_x(z)
            self.first = send(own, own, inner)
            self.begin_flow("a")

        def start_z(self):
            self.begin_flow("z")
            own = self.own_z(z)
            self.side.append((0, send(own, own, inner)))

        def start_nbr(self):
            self.first.wait_recv()
            self.begin_flow("b")

        def step(self, d):
            for f in ("a", "z", "b"):
                for way in (0, 1):
                    limit = self.hops[f][way]
                    if d > limit:
                        continue
                    self.ring[f, way, d].wait_recv()
                    where = (z + NZ - d) % NZ if way == 0 else (z + d) % NZ
                    part = self.parts[f](where)
                    if d < limit:
                        self.ring[f, way, d + 1] = send(part, part, up if way == 0 else down)
                    if f == "z":
                        self.side.append((d, send(part, part, inner)))

        def wait_side(self, low, high):
            for d, copy in self.side:
                if low <= d <= high:
                    copy.wait_recv()

    def rows(ref, start, count, by):
        return ref.at[pl.ds(aligned(start, by), count)]

    kv = Round(
        lambda w: rows(wk, 192 * (p * NZ + w), 192, 64),
        lambda w: rows(wk, 192 * ((1 - p) * NZ + w), 192, 64),
        lambda w: rows(wv, 192 * (p * NZ + w), 192, 64),
        {"a": (4, 3), "b": (3, 4), "z": (4, 3)},
    )
    qr = Round(
        lambda w: rows(wq, 192 * (p * NZ + w), 96, 32),
        lambda w: rows(wq, 192 * ((1 - p) * NZ + w), 96, 32),
        lambda w: rows(wq, 192 * (p * NZ + w) + 96, 96, 32),
        {"a": (4, 3), "b": (3, 4), "z": (3, 4)},
    )
    columns = {"x": x, "e": xe, "i": xi, "d": 3 - xi}

    def o_top(f, w):
        return rows(wo, 128 * (columns[f] * NZ + w), O_X, 16)

    def o_rest(f, w):
        return rows(wo, 128 * (columns[f] * NZ + w) + O_X, 128 - O_X, 16)

    class OutRound:
        hops = {"z": (4, 3), "x": (3, 4), "e": (4, 3), "i": (3, 4), "d": (4, 3)}

        def __init__(self):
            self.ring = {}
            self.to_inner = {}
            self.to_across = {}
            self.diagonal = {}

        def part(self, f, w):
            return o_rest("x", w) if f == "z" else o_top(f, w)

        def begin(self, f, source=None):
            part = self.part(f, z)
            source = part if source is None else source
            self.ring[f, 0, 1] = send(source, part, up)
            self.ring[f, 1, 1] = send(source, part, down)

        def sides(self, d, way, w):
            part = self.part("z", w)
            self.to_inner[d, way] = send(part, part, inner)
            self.to_across[d, way] = send(part, part, across_chip)

        def early(self):
            top, rest = wo_hbm.at[pl.ds(0, O_X)], wo_hbm.at[pl.ds(O_X, 128 - O_X)]
            self.swap = send(top, o_top("x", z), across_chip)
            self.begin("z", rest)
            self.begin("x", top)

        def exchange(self):
            self.sides(0, 1, z)
            self.tops = []
            for f in ("x", "e"):
                part = o_top(f, z)
                self.tops.append(send(part, part, inner))

        def start(self):
            self.begin("e")
            self.step(1, "zx")

        def start_nbr(self):
            for f, copy in zip(("i", "d"), self.tops):
                copy.wait_recv()
                self.begin(f)

        def step(self, d, flows):
            for f in flows:
                for way in (0, 1):
                    limit = self.hops[f][way]
                    if d > limit:
                        continue
                    self.ring[f, way, d].wait_recv()
                    w = (z + NZ - d) % NZ if way == 0 else (z + d) % NZ
                    part = self.part(f, w)
                    if d < limit:
                        self.ring[f, way, d + 1] = send(part, part, up if way == 0 else down)
                    if f == "z":
                        self.sides(d, way, w)

        def turn(self, d):
            for way in (0, 1):
                if (d, way) not in self.to_inner:
                    continue
                w = (z + NZ - d) % NZ if way == 0 else (z + d) % NZ
                self.to_inner[d, way].wait_recv()
                if way == 0:
                    part = o_rest("i", w)
                    self.diagonal[d, way] = send(part, part, across_chip)
                self.to_across[d, way].wait_recv()
                if way == 1:
                    part = o_rest("e", w)
                    self.diagonal[d, way] = send(part, part, inner)

        def wait_turned(self, low, high):
            for (d, way), copy in self.diagonal.items():
                if low <= d <= high:
                    copy.wait_recv()

    orr = OutRound()

    weights = {0: wk, 1: wv, 2: wq}
    last_pair = ((z + 4) % NZ) // 2

    def mm_chunk(which, pair):
        low = aligned(384 * pair, 128)
        high = aligned(1536 + 384 * pair, 128)
        for i in which:
            w = weights[i]
            wcat = jnp.concatenate([w[pl.ds(low, 384)], w[pl.ds(high, 384)]], axis=0)
            for j in (0, 1):
                xcat = jnp.concatenate([xs[j, :, pl.ds(low, 384)], xs[j, :, pl.ds(high, 384)]], axis=1)
                acc[i, j] += jnp.dot(xcat, wcat, preferred_element_type=F32)

    def mm_three(which):
        @pl.loop(0, 3)
        def _(m):
            mm_chunk(which, (last_pair + 1 + m) % 4)

    orr.early()
    wait_own("k")
    kv.start_x()
    wait_own("v")
    kv.start_z()
    acc[...] = jnp.zeros_like(acc)
    kv.start_nbr()
    x_local.wait()

    wait_own("aux")
    t_col = lax.broadcasted_iota(jnp.int32, (512, 128), 0)
    lane = lax.broadcasted_iota(jnp.int32, (512, 128), 1)
    cs = jnp.zeros((512, 1), F32)
    for b in range(4):
        surge = jnp.broadcast_to(aux[b : b + 1, :], (512, 128))
        cs += jnp.sum(jnp.where(lane + 128 * b <= t_col, surge, 0.0), axis=1, keepdims=True)
    cs_row = jnp.broadcast_to(cs, (512, 128)).T[0:1, :]
    total = cs[511:512, :]
    steps = lax.broadcasted_iota(jnp.int32, (512, 1), 0).astype(F32)
    t_idx = lax.broadcasted_iota(jnp.int32, (512, 512), 0)
    s_idx = lax.broadcasted_iota(jnp.int32, (512, 512), 1)
    causal = t_idx >= s_idx
    apart = (t_idx - s_idx).astype(F32)
    spread = jnp.broadcast_to(cs, (512, 512)) - jnp.broadcast_to(cs_row, (512, 512))
    for h in range(4):
        speed = aux[8 + h : 9 + h, 0:1]
        exponent = jnp.where(causal, spread - apart * speed, 0.0)
        decay[h] = jnp.where(causal, jnp.exp(exponent), 0.0)
    tot_out[...] = jnp.broadcast_to(total, (8, 128))
    totals[z] = jnp.broadcast_to(total, (8, 128))
    tot_copies = [send(tot_out, totals.at[z], z_dev[d]) for d in range(1, NZ)]

    kv.step(1)
    wait_own("q")

    theirs = 1 - region

    def x_rows(cy, start, count):
        return xs.at[theirs, pl.ds(aligned(128 * cy + start, 64), count)]

    x_up, x_down = [None, None], [None, None]
    for i in (0, 1):
        x_cross[i].wait_recv()
        mine = x_rows(y, 64 * i, 64)
        x_up[i] = send(mine, mine, y_up)
        x_down[i] = send(mine, mine, y_down)
    kv.step(2)
    x_up[0].wait_recv()
    far = x_rows((y + 3) % NY, 0, 64)
    x_up2 = send(far, far, y_up)
    x_down[1].wait_recv()
    far = x_rows((y + 1) % NY, 64, 64)
    x_down2 = send(far, far, y_down)
    kv.step(3)
    qr.start_x()
    qr.start_z()
    for copy in (x_up[1], x_down[0], x_up2, x_down2):
        copy.wait_recv()
    kv.wait_side(0, 3)
    qr.start_nbr()
    mm_chunk((0, 1), (last_pair + 1) % 4)
    kv.step(4)

    @pl.loop(2, 4)
    def _(m):
        mm_chunk((0, 1), (last_pair + m) % 4)

    qr.step(1)
    kv.wait_side(4, 4)
    mm_chunk((0,), last_pair)
    k_part = send(acc.at[0, 1 - c], part.at[0], other)
    mm_chunk((1,), last_pair)
    v_part = send(acc.at[1, 1 - c], part.at[1], other)

    k_part.wait_recv()
    ksum = acc[0, c] + part[0]
    kb[...] = (ksum * (1.0 / (1.0 + jnp.exp(-ksum)))).astype(BF16)
    v_part.wait_recv()
    vb[...] = (acc[1, c] + part[1]).astype(BF16)
    for h in range(4):
        speed = aux[8 + h : 9 + h, 0:1]
        remain = jnp.exp((total - cs) - (511.0 - steps) * speed)
        kd = (kb[:, 128 * h : 128 * h + 128].astype(F32) * remain).astype(BF16)
        state = lax.dot_general(
            kd, vb[:, 128 * h : 128 * h + 128], (((0,), (0,)), ((), ())),
            preferred_element_type=F32,
        ).astype(BF16)
        states[2 * h] = state[0:64]
        states[2 * h + 1] = state[64:128]
    arrived[z] = states[z]
    state_copies = [
        send(states.at[(z + d) % NZ], arrived.at[z], z_dev[d]) for d in range(1, NZ)
    ]
    qr.step(2)
    o_local.wait()
    orr.swap.wait_recv()
    orr.exchange()
    qr.step(3)
    orr.start()
    qr.wait_side(0, 3)
    for copy in state_copies + tot_copies:
        copy.wait_recv()
    slice_speed = aux[pl.ds(8 + z // 2, 1), 0:1]
    run = jnp.zeros((64, 128), F32)
    run_tot = jnp.zeros((1, 1), F32)
    before = []
    for w in range(NZ):
        before.append((run, run_tot))
        tot = totals[w, 0:1, 0:1]
        run = jnp.exp(tot - 512.0 * slice_speed) * run + arrived[w].astype(F32)
        run_tot = run_tot + tot
    group_out[0:64, :] = run
    group_out[64:72, :] = jnp.broadcast_to(run_tot, (8, 128))
    groups[xt] = group_out[...]
    group_copies = [send(group_out, groups.at[xt], d) for d in (other, inner, inner_other)]
    mm_three((2,))
    orr.start_nbr()
    for copy in group_copies:
        copy.wait_recv()
    carry = jnp.zeros((64, 128), F32)
    for g in range(4):
        tot = groups[g, 64:65, 0:1]
        later = jnp.exp(tot - 4096.0 * slice_speed) * carry + groups[g, 0:64, :]
        carry = jnp.where(jnp.full((64, 128), g, jnp.int32) < xt, later, carry)
    for w in range(NZ):
        run, run_tot = before[w]
        prefix_out[w] = (run + jnp.exp(run_tot - (512.0 * w) * slice_speed) * carry).astype(BF16)
    prefix[z] = prefix_out[z]
    prefix_copies = [
        send(prefix_out.at[(z + d) % NZ], prefix.at[z], z_dev[d]) for d in range(1, NZ)
    ]
    qr.step(4)
    qr.wait_side(4, 4)
    mm_chunk((2,), last_pair)
    q_part = send(acc.at[2, 1 - c], part.at[2], other)
    orr.step(1, "eid")
    orr.step(2, "zx")
    q_part.wait_recv()
    qsum = acc[2, c] + part[2]
    qb[...] = (qsum * (1.0 / (1.0 + jnp.exp(-qsum)))).astype(BF16)

    for h in range(4):
        cut = slice(128 * h, 128 * h + 128)
        scores = lax.dot_general(
            qb[:, cut], kb[:, cut], (((1,), (1,)), ((), ())), preferred_element_type=F32
        )
        acc[0, c, :, cut] = jnp.dot(
            (scores * decay[h]).astype(BF16), vb[:, cut], preferred_element_type=F32
        )
    for copy in prefix_copies:
        copy.wait_recv()
    swap_t = y * 2 + 1 - c

    def block(cy, start, count, h):
        return normed.at[cy * 2 + c, pl.ds(start, count), pl.ds(128 * h, 128)]

    ring_up, ring_down, relays, swap_copies = [], [], [], []
    for h in range(4):
        cut = slice(128 * h, 128 * h + 128)
        speed = aux[8 + h : 9 + h, 0:1]
        carried = prefix[2 * h : 2 * h + 2].reshape(128, 128)
        reach = jnp.exp(cs - (steps + 1.0) * speed)
        att = acc[0, c, :, cut] + reach * jnp.dot(qb[:, cut], carried, preferred_element_type=F32)
        square = jnp.mean(att * att, axis=1, keepdims=True)
        value = (att * lax.rsqrt(square + 1e-05) * aux[4 + h : 5 + h, :]).astype(BF16)
        mine = block(y, 0, 512, h)
        ring_up.append(remote(mine, mine, y_up))
        ring_down.append(remote(mine, mine, y_down))
        relays.append(remote(mine, mine, other))
        back = remote(staged.at[:, pl.ds(128 * h, 128)], normed.at[swap_t, :, pl.ds(128 * h, 128)], swap)
        swap_copies.append(back)

        @pl.when(home)
        def _():
            normed[t, :, cut] = value
            ring_up[h].start()
            ring_down[h].start()
            relays[h].start()

        @pl.when(away)
        def _():
            staged[:, cut] = value
            back.start()

    sent.extend(ring_up + ring_down + relays)
    sent_away.extend(swap_copies)
    orr.step(2, "eid")
    orr.turn(0)
    orr.turn(1)
    orr.step(3, "zx")

    @pl.when(away)
    def _():
        for h in range(4):
            swap_copies[h].wait_recv()
            ring_up[h].start()
            ring_down[h].start()
            relays[h].start()

    orr.turn(2)
    ring_up2, ring_down2 = [], []
    for h in range(4):
        ring_up[h].wait_recv()
        far = block((y + 3) % NY, 0, 256, h)
        ring_up2.append(send(far, far, y_up))
        whole = block((y + 3) % NY, 0, 512, h)
        relays.append(send(whole, whole, other))
        ring_down[h].wait_recv()
        far = block((y + 1) % NY, 256, 256, h)
        ring_down2.append(send(far, far, y_down))
        whole = block((y + 1) % NY, 0, 512, h)
        relays.append(send(whole, whole, other))
        if h == 1:
            orr.step(3, "eid")
            orr.step(4, "zx")
    oacc[...] = jnp.zeros_like(oacc)
    orr.turn(3)
    orr.step(4, "eid")
    orr.turn(4)
    last_relays = []
    for h in range(4):
        ring_up2[h].wait_recv()
        far = block((y + 2) % NY, 0, 256, h)
        last_relays.append(send(far, far, other))
        ring_down2[h].wait_recv()
        far = block((y + 2) % NY, 256, 256, h)
        last_relays.append(send(far, far, other))
    orr.wait_turned(0, 4)
    for copy in relays:
        copy.wait_recv()

    def out_block(b):
        right = wo[pl.ds(aligned(512 * b, 512), 512)]
        return jnp.dot(normed[b], right, preferred_element_type=F32)

    @pl.loop(0, 6)
    def _(i):
        off = i // 2 + i // 4
        oacc[...] += out_block(((y + off) % NY) * 2 + i % 2)

    for copy in last_relays:
        copy.wait_recv()
    b = ((y + 2) % NY) * 2
    out_ref[...] = (oacc[...] + out_block(b) + out_block(b + 1)).astype(BF16)

    for copy in sent:
        copy.wait_send()

    @pl.when(away)
    def _():
        for copy in sent_away:
            copy.wait_send()
    assert used[0] <= COPIES


def local(
    event_vectors,
    question_projector,
    lookup_projector,
    content_projector,
    channel_fading_speed,
    surge_fading,
    channel_scaling_coefficient,
    final_projector,
):
    return pl.pallas_call(
        kernel,
        out_shape=jax.ShapeDtypeStruct((512, 768), BF16),
        in_specs=[pl.BlockSpec(memory_space=pl.ANY)] * 5
        + [pl.BlockSpec(memory_space=pltpu.VMEM)] * 2
        + [pl.BlockSpec(memory_space=pltpu.SMEM)],
        out_specs=pl.BlockSpec(memory_space=pltpu.VMEM),
        scratch_shapes=[
            pltpu.VMEM((2, 512, 3072), BF16),
            pltpu.VMEM((3072, 512), BF16),
            pltpu.VMEM((3072, 512), BF16),
            pltpu.VMEM((3072, 512), BF16),
            pltpu.VMEM((4096, 768), BF16),
            pltpu.VMEM((3, 2, 512, 512), F32),
            pltpu.VMEM((3, 512, 512), F32),
            pltpu.VMEM((512, 512), BF16),
            pltpu.VMEM((512, 512), BF16),
            pltpu.VMEM((512, 512), BF16),
            pltpu.VMEM((4, 512, 512), F32),
            pltpu.VMEM((16, 128), F32),
            pltpu.VMEM((16, 128), F32),
            pltpu.VMEM((8, 64, 128), BF16),
            pltpu.VMEM((8, 64, 128), BF16),
            pltpu.VMEM((8, 8, 128), F32),
            pltpu.VMEM((8, 128), F32),
            pltpu.VMEM((72, 128), F32),
            pltpu.VMEM((4, 72, 128), F32),
            pltpu.VMEM((8, 64, 128), BF16),
            pltpu.VMEM((8, 64, 128), BF16),
            pltpu.VMEM((8, 512, 512), BF16),
            pltpu.VMEM((512, 512), BF16),
            pltpu.VMEM((512, 768), F32),
            pltpu.SemaphoreType.DMA((COPIES,)),
            pltpu.SemaphoreType.DMA((COPIES,)),
            pltpu.SemaphoreType.DMA((8,)),
        ],
        compiler_params=pltpu.CompilerParams(
            collective_id=0, has_side_effects=True, vmem_limit_bytes=67043328
        ),
    )(
        event_vectors,
        question_projector,
        lookup_projector,
        content_projector,
        final_projector,
        surge_fading.reshape(4, 128),
        channel_scaling_coefficient.reshape(4, 128),
        channel_fading_speed,
    )


def solution(mesh):
    in_specs = (
        P("seq", None),
        P("seq", "tp"),
        P("seq", "tp"),
        P("seq", "tp"),
        P("tp"),
        P("seq"),
        P("tp"),
        P("seq", "tp"),
    )
    out_specs = P("seq", "tp")
    return jax.shard_map(local, mesh=mesh, in_specs=in_specs, out_specs=out_specs, check_vma=False)
```

```python
import jax
import jax.numpy as jnp
from jax import lax
from jax.experimental import pallas as pl
from jax.experimental.pallas import tpu as pltpu
from jax.sharding import PartitionSpec as P

MESH = pl.DeviceIdType.MESH
F32 = jnp.float32
BF16 = jnp.bfloat16
NZ = 8
NY = 4
COPIES = 300
O_X = 64


def aligned(value, by):
    return pl.multiple_of(value, by)


def kernel(
    x_hbm, wq_hbm, wk_hbm, wv_hbm, wo_hbm, surge_ref, scale_ref, speed_ref, out_ref,
    xs, wk, wv, wq, wo, acc, part, kb, vb, qb, decay, aux, aux_own,
    states, arrived, totals, tot_out, group_out, groups, prefix_out, prefix,
    normed, staged, oacc, ssem, rsem, lsem,
):
    s = lax.axis_index("seq")
    t = lax.axis_index("tp")
    x, z = s // NZ, s % NZ
    y, c = t // 2, t % 2
    region = x // 2
    is_home = 1 - (region + c) % 2
    xe = 3 - x
    xi = x + 1 - 2 * (x % 2)
    xt = is_home * x + (1 - is_home) * xe
    p = xt % 2
    home = is_home == 1
    away = is_home == 0

    def dev(cx, cy, cz, cc):
        return (cx * NZ + cz, cy * 2 + cc)

    z_dev = [dev(x, y, (z + d) % NZ, c) for d in range(NZ)]
    up, down = z_dev[1], z_dev[NZ - 1]
    inner = dev(xi, y, z, c)
    inner_other = dev(xi, y, z, 1 - c)
    across_chip = dev(xe, y, z, c)
    swap = dev(xe, y, z, 1 - c)
    other = dev(x, y, z, 1 - c)
    y_up = dev(x, (y + 1) % NY, z, c)
    y_down = dev(x, (y + 3) % NY, z, c)
    peers = z_dev[1:] + [inner, inner_other, across_chip, swap, other, y_up, y_down]

    used = [0]
    sent = []
    sent_away = []

    def remote(src, dst, device):
        i = used[0]
        used[0] += 1
        return pltpu.make_async_remote_copy(
            src_ref=src, dst_ref=dst, send_sem=ssem.at[i], recv_sem=rsem.at[i],
            device_id=device, device_id_type=MESH,
        )

    def send(src, dst, device):
        copy = remote(src, dst, device)
        copy.start()
        sent.append(copy)
        return copy

    aux_own[0:4, :] = surge_ref[...]
    aux_own[4:8, :] = scale_ref[...]
    for h in range(4):
        aux_own[8 + h : 9 + h, :] = jnp.full((1, 128), speed_ref[h], F32)
    aux_own[12:16, :] = jnp.zeros((4, 128), F32)

    barrier = pltpu.get_barrier_semaphore()
    for device in peers:
        pl.semaphore_signal(barrier, inc=1, device_id=device, device_id_type=MESH)
    pl.semaphore_wait(barrier, len(peers))

    own_row = aligned(192 * (p * NZ + z), 64)
    source_row = aligned(192 * ((x % 2) * NZ + z), 64)
    swaps = {}

    def own_piece(name, src, dst, index):
        local = pltpu.make_async_copy(src, dst, lsem.at[index])
        copy = remote(src, dst, swap)
        swaps[name] = (local, copy)

        @pl.when(home)
        def _():
            local.start()

        @pl.when(away)
        def _():
            copy.start()

        sent_away.append(copy)

    def wait_own(name):
        local, copy = swaps[name]

        @pl.when(home)
        def _():
            local.wait()

        @pl.when(away)
        def _():
            copy.wait_recv()

    own_piece("k", wk_hbm, wk.at[pl.ds(source_row, 192)], 0)
    own_piece("v", wv_hbm, wv.at[pl.ds(source_row, 192)], 1)
    own_piece("aux", aux_own, aux, 2)
    half_lane = aligned(3072 * c, 128)
    x_cross = []
    for i in (0, 1):
        some = pl.ds(aligned(128 * y + 64 * i, 64), 64)
        x_cross.append(
            send(x_hbm.at[some, pl.ds(half_lane, 3072)], xs.at[region, some], across_chip)
        )
    own_piece("q", wq_hbm, wq.at[pl.ds(source_row, 192)], 3)
    x_local = pltpu.make_async_copy(x_hbm.at[:, pl.ds(half_lane, 3072)], xs.at[region], lsem.at[4])
    x_local.start()
    o_own_row = aligned(128 * s, 128)
    o_local = pltpu.make_async_copy(wo_hbm, wo.at[pl.ds(o_own_row, 128)], lsem.at[5])
    o_local.start()

    class Round:
        def __init__(self, own_x, nbr_x, own_z, hops):
            self.own_x, self.nbr_x, self.own_z = own_x, nbr_x, own_z
            self.parts = {"a": own_x, "b": nbr_x, "z": own_z}
            self.hops = hops
            self.ring = {}
            self.side = []

        def begin_flow(self, f):
            part = self.parts[f](z)
            self.ring[f, 0, 1] = send(part, part, up)
            self.ring[f, 1, 1] = send(part, part, down)

        def start_x(self):
            own = self.own_x(z)
            self.first = send(own, own, inner)
            self.begin_flow("a")

        def start_z(self):
            self.begin_flow("z")
            own = self.own_z(z)
            self.side.append((0, send(own, own, inner)))

        def start_nbr(self):
            self.first.wait_recv()
            self.begin_flow("b")

        def step(self, d):
            for f in ("a", "z", "b"):
                for way in (0, 1):
                    limit = self.hops[f][way]
                    if d > limit:
                        continue
                    self.ring[f, way, d].wait_recv()
                    where = (z + NZ - d) % NZ if way == 0 else (z + d) % NZ
                    part = self.parts[f](where)
                    if d < limit:
                        self.ring[f, way, d + 1] = send(part, part, up if way == 0 else down)
                    if f == "z":
                        self.side.append((d, send(part, part, inner)))

        def wait_side(self, low, high):
            for d, copy in self.side:
                if low <= d <= high:
                    copy.wait_recv()

    def rows(ref, start, count, by):
        return ref.at[pl.ds(aligned(start, by), count)]

    kv = Round(
        lambda w: rows(wk, 192 * (p * NZ + w), 192, 64),
        lambda w: rows(wk, 192 * ((1 - p) * NZ + w), 192, 64),
        lambda w: rows(wv, 192 * (p * NZ + w), 192, 64),
        {"a": (4, 3), "b": (3, 4), "z": (4, 3)},
    )
    qr = Round(
        lambda w: rows(wq, 192 * (p * NZ + w), 96, 32),
        lambda w: rows(wq, 192 * ((1 - p) * NZ + w), 96, 32),
        lambda w: rows(wq, 192 * (p * NZ + w) + 96, 96, 32),
        {"a": (4, 3), "b": (3, 4), "z": (3, 4)},
    )
    columns = {"x": x, "e": xe, "i": xi, "d": 3 - xi}

    def o_top(f, w):
        return rows(wo, 128 * (columns[f] * NZ + w), O_X, 16)

    def o_rest(f, w):
        return rows(wo, 128 * (columns[f] * NZ + w) + O_X, 128 - O_X, 16)

    class OutRound:
        hops = {"z": (4, 3), "x": (3, 4), "e": (4, 3), "i": (3, 4), "d": (4, 3)}

        def __init__(self):
            self.ring = {}
            self.to_inner = {}
            self.to_across = {}
            self.diagonal = {}

        def part(self, f, w):
            return o_rest("x", w) if f == "z" else o_top(f, w)

        def begin(self, f, source=None):
            part = self.part(f, z)
            source = part if source is None else source
            self.ring[f, 0, 1] = send(source, part, up)
            self.ring[f, 1, 1] = send(source, part, down)

        def sides(self, d, way, w):
            part = self.part("z", w)
            self.to_inner[d, way] = send(part, part, inner)
            self.to_across[d, way] = send(part, part, across_chip)

        def early(self):
            top, rest = wo_hbm.at[pl.ds(0, O_X)], wo_hbm.at[pl.ds(O_X, 128 - O_X)]
            self.swap = send(top, o_top("x", z), across_chip)
            self.begin("z", rest)
            self.begin("x", top)

        def exchange(self):
            self.sides(0, 1, z)
            self.tops = []
            for f in ("x", "e"):
                part = o_top(f, z)
                self.tops.append(send(part, part, inner))

        def start(self):
            self.begin("e")
            self.step(1, "zx")

        def start_nbr(self):
            for f, copy in zip(("i", "d"), self.tops):
                copy.wait_recv()
                self.begin(f)

        def step(self, d, flows):
            for f in flows:
                for way in (0, 1):
                    limit = self.hops[f][way]
                    if d > limit:
                        continue
                    self.ring[f, way, d].wait_recv()
                    w = (z + NZ - d) % NZ if way == 0 else (z + d) % NZ
                    part = self.part(f, w)
                    if d < limit:
                        self.ring[f, way, d + 1] = send(part, part, up if way == 0 else down)
                    if f == "z":
                        self.sides(d, way, w)

        def turn(self, d):
            for way in (0, 1):
                if (d, way) not in self.to_inner:
                    continue
                w = (z + NZ - d) % NZ if way == 0 else (z + d) % NZ
                self.to_inner[d, way].wait_recv()
                if way == 0:
                    part = o_rest("i", w)
                    self.diagonal[d, way] = send(part, part, across_chip)
                self.to_across[d, way].wait_recv()
                if way == 1:
                    part = o_rest("e", w)
                    self.diagonal[d, way] = send(part, part, inner)

        def wait_turned(self, low, high):
            for (d, way), copy in self.diagonal.items():
                if low <= d <= high:
                    copy.wait_recv()

    orr = OutRound()

    weights = {0: wk, 1: wv, 2: wq}
    last_pair = ((z + 4) % NZ) // 2

    def mm_chunk(which, pair):
        low = aligned(384 * pair, 128)
        high = aligned(1536 + 384 * pair, 128)
        for i in which:
            w = weights[i]
            wcat = jnp.concatenate([w[pl.ds(low, 384)], w[pl.ds(high, 384)]], axis=0)
            for j in (0, 1):
                xcat = jnp.concatenate([xs[j, :, pl.ds(low, 384)], xs[j, :, pl.ds(high, 384)]], axis=1)
                acc[i, j] += jnp.dot(xcat, wcat, preferred_element_type=F32)

    def mm_three(which):
        @pl.loop(0, 3)
        def _(m):
            mm_chunk(which, (last_pair + 1 + m) % 4)

    orr.early()
    wait_own("k")
    kv.start_x()
    wait_own("v")
    kv.start_z()
    acc[...] = jnp.zeros_like(acc)
    kv.start_nbr()
    x_local.wait()

    wait_own("aux")
    t_col = lax.broadcasted_iota(jnp.int32, (512, 128), 0)
    lane = lax.broadcasted_iota(jnp.int32, (512, 128), 1)
    cs = jnp.zeros((512, 1), F32)
    for b in range(4):
        surge = jnp.broadcast_to(aux[b : b + 1, :], (512, 128))
        cs += jnp.sum(jnp.where(lane + 128 * b <= t_col, surge, 0.0), axis=1, keepdims=True)
    cs_row = jnp.broadcast_to(cs, (512, 128)).T[0:1, :]
    total = cs[511:512, :]
    steps = lax.broadcasted_iota(jnp.int32, (512, 1), 0).astype(F32)
    t_idx = lax.broadcasted_iota(jnp.int32, (512, 512), 0)
    s_idx = lax.broadcasted_iota(jnp.int32, (512, 512), 1)
    causal = t_idx >= s_idx
    apart = (t_idx - s_idx).astype(F32)
    spread = jnp.broadcast_to(cs, (512, 512)) - jnp.broadcast_to(cs_row, (512, 512))
    for h in range(4):
        speed = aux[8 + h : 9 + h, 0:1]
        exponent = jnp.where(causal, spread - apart * speed, 0.0)
        decay[h] = jnp.where(causal, jnp.exp(exponent), 0.0)
    tot_out[...] = jnp.broadcast_to(total, (8, 128))
    totals[z] = jnp.broadcast_to(total, (8, 128))
    tot_copies = [send(tot_out, totals.at[z], z_dev[d]) for d in range(1, NZ)]

    kv.step(1)
    wait_own("q")

    theirs = 1 - region

    def x_rows(cy, start, count):
        return xs.at[theirs, pl.ds(aligned(128 * cy + start, 64), count)]

    x_up, x_down = [None, None], [None, None]
    for i in (0, 1):
        x_cross[i].wait_recv()
        mine = x_rows(y, 64 * i, 64)
        x_up[i] = send(mine, mine, y_up)
        x_down[i] = send(mine, mine, y_down)
    kv.step(2)
    x_up[0].wait_recv()
    far = x_rows((y + 3) % NY, 0, 64)
    x_up2 = send(far, far, y_up)
    x_down[1].wait_recv()
    far = x_rows((y + 1) % NY, 64, 64)
    x_down2 = send(far, far, y_down)
    kv.step(3)
    qr.start_x()
    qr.start_z()
    for copy in (x_up[1], x_down[0], x_up2, x_down2):
        copy.wait_recv()
    kv.wait_side(0, 3)
    qr.start_nbr()
    mm_chunk((0, 1), (last_pair + 1) % 4)
    kv.step(4)

    @pl.loop(2, 4)
    def _(m):
        mm_chunk((0, 1), (last_pair + m) % 4)

    qr.step(1)
    kv.wait_side(4, 4)
    mm_chunk((0,), last_pair)
    k_part = send(acc.at[0, 1 - c], part.at[0], other)
    mm_chunk((1,), last_pair)
    v_part = send(acc.at[1, 1 - c], part.at[1], other)

    k_part.wait_recv()
    ksum = acc[0, c] + part[0]
    kb[...] = (ksum * (1.0 / (1.0 + jnp.exp(-ksum)))).astype(BF16)
    v_part.wait_recv()
    vb[...] = (acc[1, c] + part[1]).astype(BF16)
    for h in range(4):
        speed = aux[8 + h : 9 + h, 0:1]
        remain = jnp.exp((total - cs) - (511.0 - steps) * speed)
        kd = (kb[:, 128 * h : 128 * h + 128].astype(F32) * remain).astype(BF16)
        state = lax.dot_general(
            kd, vb[:, 128 * h : 128 * h + 128], (((0,), (0,)), ((), ())),
            preferred_element_type=F32,
        ).astype(BF16)
        states[2 * h] = state[0:64]
        states[2 * h + 1] = state[64:128]
    arrived[z] = states[z]
    state_copies = [
        send(states.at[(z + d) % NZ], arrived.at[z], z_dev[d]) for d in range(1, NZ)
    ]
    qr.step(2)
    o_local.wait()
    orr.swap.wait_recv()
    orr.exchange()
    qr.step(3)
    orr.start()
    qr.wait_side(0, 3)
    for copy in state_copies + tot_copies:
        copy.wait_recv()
    slice_speed = aux[pl.ds(8 + z // 2, 1), 0:1]
    run = jnp.zeros((64, 128), F32)
    run_tot = jnp.zeros((1, 1), F32)
    before = []
    for w in range(NZ):
        before.append((run, run_tot))
        tot = totals[w, 0:1, 0:1]
        run = jnp.exp(tot - 512.0 * slice_speed) * run + arrived[w].astype(F32)
        run_tot = run_tot + tot
    group_out[0:64, :] = run
    group_out[64:72, :] = jnp.broadcast_to(run_tot, (8, 128))
    groups[xt] = group_out[...]
    group_copies = [send(group_out, groups.at[xt], d) for d in (other, inner, inner_other)]
    mm_three((2,))
    orr.start_nbr()
    for copy in group_copies:
        copy.wait_recv()
    carry = jnp.zeros((64, 128), F32)
    for g in range(4):
        tot = groups[g, 64:65, 0:1]
        later = jnp.exp(tot - 4096.0 * slice_speed) * carry + groups[g, 0:64, :]
        carry = jnp.where(jnp.full((64, 128), g, jnp.int32) < xt, later, carry)
    for w in range(NZ):
        run, run_tot = before[w]
        prefix_out[w] = (run + jnp.exp(run_tot - (512.0 * w) * slice_speed) * carry).astype(BF16)
    prefix[z] = prefix_out[z]
    prefix_copies = [
        send(prefix_out.at[(z + d) % NZ], prefix.at[z], z_dev[d]) for d in range(1, NZ)
    ]
    qr.step(4)
    qr.wait_side(4, 4)
    mm_chunk((2,), last_pair)
    q_part = send(acc.at[2, 1 - c], part.at[2], other)
    orr.step(1, "eid")
    orr.step(2, "zx")
    q_part.wait_recv()
    qsum = acc[2, c] + part[2]
    qb[...] = (qsum * (1.0 / (1.0 + jnp.exp(-qsum)))).astype(BF16)

    for h in range(4):
        cut = slice(128 * h, 128 * h + 128)
        scores = lax.dot_general(
            qb[:, cut], kb[:, cut], (((1,), (1,)), ((), ())), preferred_element_type=F32
        )
        acc[0, c, :, cut] = jnp.dot(
            (scores * decay[h]).astype(BF16), vb[:, cut], preferred_element_type=F32
        )
    for copy in prefix_copies:
        copy.wait_recv()
    swap_t = y * 2 + 1 - c

    def block(cy, start, count, h):
        return normed.at[cy * 2 + c, pl.ds(start, count), pl.ds(128 * h, 128)]

    ring_up, ring_down, relays, swap_copies = [], [], [], []
    for h in range(4):
        cut = slice(128 * h, 128 * h + 128)
        speed = aux[8 + h : 9 + h, 0:1]
        carried = prefix[2 * h : 2 * h + 2].reshape(128, 128)
        reach = jnp.exp(cs - (steps + 1.0) * speed)
        att = acc[0, c, :, cut] + reach * jnp.dot(qb[:, cut], carried, preferred_element_type=F32)
        square = jnp.mean(att * att, axis=1, keepdims=True)
        value = (att * lax.rsqrt(square + 1e-05) * aux[4 + h : 5 + h, :]).astype(BF16)
        mine = block(y, 0, 512, h)
        ring_up.append(remote(mine, mine, y_up))
        ring_down.append(remote(mine, mine, y_down))
        relays.append(remote(mine, mine, other))
        back = remote(staged.at[:, pl.ds(128 * h, 128)], normed.at[swap_t, :, pl.ds(128 * h, 128)], swap)
        swap_copies.append(back)

        @pl.when(home)
        def _():
            normed[t, :, cut] = value
            ring_up[h].start()
            ring_down[h].start()
            relays[h].start()

        @pl.when(away)
        def _():
            staged[:, cut] = value
            back.start()

    sent.extend(ring_up + ring_down + relays)
    sent_away.extend(swap_copies)
    orr.step(2, "eid")
    orr.turn(0)
    orr.turn(1)
    @pl.when(away)
    def _():
        for h in range(4):
            swap_copies[h].wait_recv()
            ring_up[h].start()
            ring_down[h].start()
            relays[h].start()

    orr.step(3, "zx")

    orr.turn(2)
    ring_up2, ring_down2 = [], []
    for h in range(4):
        ring_up[h].wait_recv()
        far = block((y + 3) % NY, 0, 256, h)
        ring_up2.append(send(far, far, y_up))
        whole = block((y + 3) % NY, 0, 512, h)
        relays.append(send(whole, whole, other))
        ring_down[h].wait_recv()
        far = block((y + 1) % NY, 256, 256, h)
        ring_down2.append(send(far, far, y_down))
        whole = block((y + 1) % NY, 0, 512, h)
        relays.append(send(whole, whole, other))
        if h == 1:
            orr.step(3, "eid")
            orr.step(4, "zx")
    oacc[...] = jnp.zeros_like(oacc)
    orr.turn(3)
    orr.step(4, "eid")
    orr.turn(4)
    last_relays = []
    for h in range(4):
        ring_up2[h].wait_recv()
        far = block((y + 2) % NY, 0, 256, h)
        last_relays.append(send(far, far, other))
        ring_down2[h].wait_recv()
        far = block((y + 2) % NY, 256, 256, h)
        last_relays.append(send(far, far, other))
    orr.wait_turned(0, 4)
    for copy in relays:
        copy.wait_recv()

    def out_block(b):
        right = wo[pl.ds(aligned(512 * b, 512), 512)]
        return jnp.dot(normed[b], right, preferred_element_type=F32)

    @pl.loop(0, 6)
    def _(i):
        off = i // 2 + i // 4
        oacc[...] += out_block(((y + off) % NY) * 2 + i % 2)

    for copy in last_relays:
        copy.wait_recv()
    b = ((y + 2) % NY) * 2
    out_ref[...] = (oacc[...] + out_block(b) + out_block(b + 1)).astype(BF16)

    for copy in sent:
        copy.wait_send()

    @pl.when(away)
    def _():
        for copy in sent_away:
            copy.wait_send()
    assert used[0] <= COPIES


def local(
    event_vectors,
    question_projector,
    lookup_projector,
    content_projector,
    channel_fading_speed,
    surge_fading,
    channel_scaling_coefficient,
    final_projector,
):
    return pl.pallas_call(
        kernel,
        out_shape=jax.ShapeDtypeStruct((512, 768), BF16),
        in_specs=[pl.BlockSpec(memory_space=pl.ANY)] * 5
        + [pl.BlockSpec(memory_space=pltpu.VMEM)] * 2
        + [pl.BlockSpec(memory_space=pltpu.SMEM)],
        out_specs=pl.BlockSpec(memory_space=pltpu.VMEM),
        scratch_shapes=[
            pltpu.VMEM((2, 512, 3072), BF16),
            pltpu.VMEM((3072, 512), BF16),
            pltpu.VMEM((3072, 512), BF16),
            pltpu.VMEM((3072, 512), BF16),
            pltpu.VMEM((4096, 768), BF16),
            pltpu.VMEM((3, 2, 512, 512), F32),
            pltpu.VMEM((3, 512, 512), F32),
            pltpu.VMEM((512, 512), BF16),
            pltpu.VMEM((512, 512), BF16),
            pltpu.VMEM((512, 512), BF16),
            pltpu.VMEM((4, 512, 512), F32),
            pltpu.VMEM((16, 128), F32),
            pltpu.VMEM((16, 128), F32),
            pltpu.VMEM((8, 64, 128), BF16),
            pltpu.VMEM((8, 64, 128), BF16),
            pltpu.VMEM((8, 8, 128), F32),
            pltpu.VMEM((8, 128), F32),
            pltpu.VMEM((72, 128), F32),
            pltpu.VMEM((4, 72, 128), F32),
            pltpu.VMEM((8, 64, 128), BF16),
            pltpu.VMEM((8, 64, 128), BF16),
            pltpu.VMEM((8, 512, 512), BF16),
            pltpu.VMEM((512, 512), BF16),
            pltpu.VMEM((512, 768), F32),
            pltpu.SemaphoreType.DMA((COPIES,)),
            pltpu.SemaphoreType.DMA((COPIES,)),
            pltpu.SemaphoreType.DMA((8,)),
        ],
        compiler_params=pltpu.CompilerParams(
            collective_id=0, has_side_effects=True, vmem_limit_bytes=67043328
        ),
    )(
        event_vectors,
        question_projector,
        lookup_projector,
        content_projector,
        final_projector,
        surge_fading.reshape(4, 128),
        channel_scaling_coefficient.reshape(4, 128),
        channel_fading_speed,
    )


def solution(mesh):
    in_specs = (
        P("seq", None),
        P("seq", "tp"),
        P("seq", "tp"),
        P("seq", "tp"),
        P("tp"),
        P("seq"),
        P("tp"),
        P("seq", "tp"),
    )
    out_specs = P("seq", "tp")
    return jax.shard_map(local, mesh=mesh, in_specs=in_specs, out_specs=out_specs, check_vma=False)
```
